32 devices in a mesh: groups: 2 (over x), gx: 16 (over z, y, core).
Axes of the slice: x: 2, y: 2, z: 4, core: 2. Of those that a mesh axis runs over, the one named last changes fastest.
Arguments:
- features: bfloat16 [128, 8, 8, 8, 128], P(('groups', 'gx')), parts along dimension 0, may hold values from -6 to 6
- fine_nbr: int32 [128, 27], P(('groups', 'gx')), parts along dimension 0, may hold values from -1 to 3, as said below
- fine_send: int32 [32, 2, 4], P(('groups', 'gx')), parts along dimension 0, may hold values from -1 to 3, as said below
- fine_parent: int32 [128], P(('groups', 'gx')), parts along dimension 0, may hold values from -1 to 127, as said below
- coarse_child: int32 [32, 8], P(('groups', 'gx')), parts along dimension 0, may hold values from -1 to 63, as said below
- coarse_nbr: int32 [32, 27], P(('groups', 'gx')), parts along dimension 0, may hold values from -1 to 15, as said below
- enc_fine_w: bfloat16 [27, 128, 128], replicated, may hold values from -0.15625 to 0.15625
- enc_coarse_w: bfloat16 [27, 128, 128], replicated, may hold values from -0.15625 to 0.15625
- dec_coarse_w: bfloat16 [27, 128, 128], replicated, may hold values from -0.15625 to 0.15625
- dec_fine_w: bfloat16 [27, 128, 128], replicated, may hold values from -0.15625 to 0.15625
Outputs:
- fine_out: bfloat16 [128, 8, 8, 8, 128], P(('groups', 'gx')), parts along dimension 0
The draws below stay inside these ranges and needn't reach their ends.
There are 2 independent parts, one for each index of `groups`. The reference program is written for one: setup_inputs(seed, part) draws one part's arguments, and reference() takes and returns one part's arrays. A program takes and returns all parts, laid end to end along the dimension named above; an argument that names none is the same for every part. Nothing has to cross between parts.
Inputs may be any that keep to these rules, and one draw needn't show every extreme that they name: `fine_nbr`: entry t of a fine slot on gx device d names the slot, on device d + dx, of the brick at brick offset (dx, dy, dz), or is -1 where there is none. A slot whose entry 13 is -1 holds no brick and all its entries are -1; entry 13 of a brick is its own slot. Adjacency is symmetric. `fine_send`: on device d, entry s of row 0 is s when slot s holds a brick with a neighbour on device d + 1, else -1; row 1 likewise for device d - 1. `fine_parent`: 8 g + o for a brick whose parent is coarse slot g at octant o, -1 for slots without a brick. Coarse slot g is held by gx device g, which lies in the same aligned group of four gx devices as the child's device. `coarse_child`: entry o of coarse slot g is the fine slot f with fine_parent[f] = 8 g + o, or -1 where there is none. `coarse_nbr`: entry t (taps ordered as for fine_nbr) is the coarse slot of the neighbouring coarse brick, or -1 where there is none; entry 13 is the brick's own slot; every neighbour is held by a gx device of the same or an adjacent aligned group of four, and neighbours with dx = 0 by a device of the same aligned group of four.
All inputs are finite; a program needn't handle non-finite values.
Results may differ from the reference program's by a relative error of at most 0.01.
Values may be sent and summed in bfloat16 or wider, within the bound.
A program may use at most 128 MiB of HBM per device.

```python
import jax
import jax.numpy as jnp
import numpy as np
from jax import lax

C = 128
EDGE = 8
FB = 4
CB = 1
NF = 64
NC = 16
N_GX = 16


OFFSETS = (-1, 0, 1)


def geometry(key):
    keys = jax.random.split(jax.random.fold_in(key, 7), 6)
    columns = N_GX
    depth = FB // 2
    places = 2 * FB
    tap_x = jnp.asarray(np.repeat(np.array(OFFSETS), 9), jnp.int32)
    tap_y = jnp.asarray(np.tile(np.repeat(np.array(OFFSETS), 3), 3), jnp.int32)
    tap_z = jnp.asarray(np.tile(np.array(OFFSETS), 9), jnp.int32)
    counts = jax.random.randint(keys[0], (columns,), FB // 2, FB + 1)
    busiest = jax.random.randint(keys[1], (), 0, columns)
    counts = jnp.where(jnp.arange(columns) == busiest, FB, counts)
    place_order = jax.vmap(lambda sub: jax.random.permutation(sub, places))(jax.random.split(keys[2], columns))
    slot_order = jax.vmap(lambda sub: jax.random.permutation(sub, FB))(jax.random.split(keys[3], columns))
    rank = jnp.arange(FB, dtype=jnp.int32)
    live_place = jnp.where(rank[None, :] < counts[:, None], place_order[:, :FB], -1).astype(jnp.int32)
    column_ids = jnp.arange(columns, dtype=jnp.int32)[:, None]
    slot_place = jnp.full((columns, FB), -1, jnp.int32).at[column_ids, slot_order].set(live_place)
    target = jnp.where(slot_place >= 0, slot_place, places)
    place_slot = jnp.full((columns, places + 1), -1, jnp.int32).at[column_ids, target].set(jnp.broadcast_to(rank, (columns, FB)))[:, :places]
    live = slot_place >= 0
    fine_y = jnp.where(live, slot_place // depth, 0)
    fine_z = jnp.where(live, slot_place % depth, 0)
    near_x = column_ids[:, :, None] + tap_x
    near_y = fine_y[:, :, None] + tap_y
    near_z = fine_z[:, :, None] + tap_z
    inside = live[:, :, None] & (near_x >= 0) & (near_x < columns) & (near_y >= 0) & (near_y < 4)
    inside = inside & (near_z >= 0) & (near_z < depth)
    found = place_slot[jnp.clip(near_x, 0, columns - 1), jnp.clip(near_y, 0, 3) * depth + jnp.clip(near_z, 0, depth - 1)]
    fine_nbr = jnp.where(inside, found, -1).astype(jnp.int32)
    upward = jnp.any(fine_nbr[:, :, 18:] >= 0, axis=-1)
    downward = jnp.any(fine_nbr[:, :, :9] >= 0, axis=-1)
    fine_send = jnp.stack([jnp.where(upward, rank, -1), jnp.where(downward, rank, -1)], axis=1).astype(jnp.int32)
    quads = columns // 4
    coarse_depth = FB // 4
    coarse_order = jax.vmap(lambda sub: jax.random.permutation(sub, FB))(jax.random.split(keys[4], quads))

    def coarse_slot(coarse_x, coarse_y, coarse_z):
        local = coarse_x % 2 * (FB // 2) + coarse_y * coarse_depth + coarse_z
        return coarse_x // 2 * FB + coarse_order[coarse_x // 2, local]
    parent_x = column_ids // 2
    parent = coarse_slot(jnp.broadcast_to(parent_x, (columns, FB)), fine_y // 2, fine_z // 2)
    octant = column_ids % 2 * 4 + fine_y % 2 * 2 + fine_z % 2
    fine_parent = jnp.where(live, parent * 8 + octant, -1).astype(jnp.int32).reshape(NF)
    dump = NC * 8
    coarse_child = jnp.full((NC * 8 + 1,), -1, jnp.int32).at[jnp.where(fine_parent >= 0, fine_parent, dump)].set(jnp.arange(NF, dtype=jnp.int32))[:NC * 8].reshape(NC, 8)
    width_x = columns // 2
    grid_x = jnp.broadcast_to(jnp.arange(width_x, dtype=jnp.int32)[:, None, None], (width_x, 2, coarse_depth))
    grid_y = jnp.broadcast_to(jnp.arange(2, dtype=jnp.int32)[None, :, None], (width_x, 2, coarse_depth))
    grid_z = jnp.broadcast_to(jnp.arange(coarse_depth, dtype=jnp.int32)[None, None, :], (width_x, 2, coarse_depth))
    step_x = grid_x[..., None] + tap_x
    step_y = grid_y[..., None] + tap_y
    step_z = grid_z[..., None] + tap_z
    within = (step_x >= 0) & (step_x < width_x) & (step_y >= 0) & (step_y < 2) & (step_z >= 0) & (step_z < coarse_depth)
    neighbour = coarse_slot(jnp.clip(step_x, 0, width_x - 1), jnp.clip(step_y, 0, 1), jnp.clip(step_z, 0, coarse_depth - 1))
    neighbour = jnp.where(within, neighbour, -1).astype(jnp.int32).reshape(-1, 27)
    owners = coarse_slot(grid_x, grid_y, grid_z).reshape(-1)
    coarse_nbr = jnp.zeros((NC, 27), jnp.int32).at[owners].set(neighbour)
    return (fine_nbr.reshape(NF, 27), fine_send, fine_parent, coarse_child, coarse_nbr)


def draw_fine_nbr(key, part):
    return geometry(key)[0]


def draw_fine_send(key, part):
    return geometry(key)[1]


def draw_fine_parent(key, part):
    return geometry(key)[2]


def draw_coarse_child(key, part):
    return geometry(key)[3]


def draw_coarse_nbr(key, part):
    return geometry(key)[4]


def block_levels(key, extent, pieces, least, top_value):
    level, own = 1.0, jax.random.fold_in(key, 6)
    for axis_at, blocks in pieces:
        steps = jnp.exp(jax.random.uniform(jax.random.fold_in(own, axis_at), (blocks,), jnp.float32, least / len(pieces), top_value / len(pieces)))
        level = level * jnp.repeat(steps, extent[axis_at] // blocks).reshape([-1 if axis == axis_at else 1 for axis in range(len(extent))])
    return level


def scatter_about(stream_key, shape, scale, most, cuts=(), kind=jnp.bfloat16):
    values = jax.random.normal(stream_key, shape, jnp.float32) * scale
    if len(cuts) > 0:
        values = block_levels(stream_key, shape, cuts, -0.22, 0.18) * values
    return jnp.clip(values, min=-most, max=most).astype(kind)


def setup_inputs(seed: int = 0, part: int = 0) -> dict:
    seeds = jax.random.split(jax.random.key(seed), 11)
    part_keys = jax.random.split(jax.random.fold_in(seeds[10], part), 11)
    features = scatter_about(part_keys[0], (NF, EDGE, EDGE, EDGE, C), 1.0, 6.0, ((0, 16),))
    fine_nbr = draw_fine_nbr(jax.random.fold_in(jax.random.fold_in(seeds[10], part), 71), part)
    fine_send = draw_fine_send(jax.random.fold_in(jax.random.fold_in(seeds[10], part), 71), part)
    fine_parent = draw_fine_parent(jax.random.fold_in(jax.random.fold_in(seeds[10], part), 71), part)
    coarse_child = draw_coarse_child(jax.random.fold_in(jax.random.fold_in(seeds[10], part), 71), part)
    coarse_nbr = draw_coarse_nbr(jax.random.fold_in(jax.random.fold_in(seeds[10], part), 71), part)
    enc_fine_w = scatter_about(seeds[6], (27, C, C), (27 * C // 2) ** -0.5, 0.15625)
    enc_coarse_w = scatter_about(seeds[7], (27, C, C), (27 * C // 2) ** -0.5, 0.15625)
    dec_coarse_w = scatter_about(seeds[8], (27, C, C), (27 * C // 2) ** -0.5, 0.15625)
    dec_fine_w = scatter_about(seeds[9], (27, C, C), (27 * C // 2) ** -0.5, 0.15625)
    return dict(features=features, fine_nbr=fine_nbr, fine_send=fine_send, fine_parent=fine_parent, coarse_child=coarse_child, coarse_nbr=coarse_nbr, enc_fine_w=enc_fine_w, enc_coarse_w=enc_coarse_w, dec_coarse_w=dec_coarse_w, dec_fine_w=dec_fine_w)


OFFSETS = (-1, 0, 1)


def region(offset, edge):
    if offset < 0:
        return slice(edge - 1, edge)
    if offset == 0:
        return slice(0, edge)
    return slice(0, 1)


def assemble(tables, index, edge):
    layers = []
    for offset_x in OFFSETS:
        table = tables[offset_x + 1]
        rows = []
        for offset_y in OFFSETS:
            cells = []
            for offset_z in OFFSETS:
                tap = 9 * (offset_x + 1) + 3 * (offset_y + 1) + offset_z + 1
                piece = table[:, :, region(offset_y, edge), region(offset_z, edge), :]
                cells.append(jnp.take(piece, index[:, tap], axis=0))
            rows.append(jnp.concatenate(cells, axis=3))
        layers.append(jnp.concatenate(rows, axis=2))
    return jnp.concatenate(layers, axis=1)


def convolve(padded, weights, edge):
    count = padded.shape[0]
    width = padded.shape[-1]
    total = jnp.zeros((count * edge ** 3, width), jnp.float32)
    for first in range(3):
        columns = jnp.concatenate([padded[:, first:first + edge, second:second + edge, third:third + edge, :]
                                   for second in range(3) for third in range(3)], axis=-1)
        columns = columns.reshape(count * edge ** 3, 9 * width).astype(jnp.float32)
        kernel = weights[9 * first:9 * first + 9].reshape(9 * width, width).astype(jnp.float32)
        total = total + jnp.dot(columns, kernel, preferred_element_type=jnp.float32)
    return jax.nn.relu(total).astype(jnp.bfloat16).reshape(count, edge, edge, edge, width)


def layer(bricks, index, weights, block):
    edge = bricks.shape[1]
    width = bricks.shape[-1]
    table = jnp.concatenate([bricks, jnp.zeros((1,) + bricks.shape[1:], jnp.bfloat16)], axis=0)
    tables = [table[:, edge - 1:], table, table[:, :1]]
    blocks = index.reshape(-1, block, 27)
    result = lax.map(lambda part_index: convolve(assemble(tables, part_index, edge), weights, edge), blocks)
    return result.reshape(-1, edge, edge, edge, width)


def from_octants(blocks, half):
    count = blocks.shape[0]
    width = blocks.shape[-1]
    shaped = blocks.reshape(count, 2, 2, 2, half, half, half, width).transpose(0, 1, 4, 2, 5, 3, 6, 7)
    return shaped.reshape(count, 2 * half, 2 * half, 2 * half, width)


def to_octants(bricks, half):
    count = bricks.shape[0]
    width = bricks.shape[-1]
    shaped = bricks.reshape(count, 2, half, 2, half, 2, half, width).transpose(0, 1, 3, 5, 2, 4, 6, 7)
    return shaped.reshape(count * 8, half, half, half, width)


def reference(features, fine_nbr, fine_send, fine_parent, coarse_child, coarse_nbr,
              enc_fine_w, enc_coarse_w, dec_coarse_w, dec_fine_w):
    edge = features.shape[1]
    width = features.shape[-1]
    half = edge // 2
    tap_x = jnp.asarray(np.repeat(np.array(OFFSETS), 9), jnp.int32)
    slot = jnp.arange(NF, dtype=jnp.int32)
    device = slot // FB
    neighbour_device = device[:, None] + tap_x[None, :]
    target = neighbour_device * FB + fine_nbr
    row = jnp.where(tap_x > 0, 1, 0).astype(jnp.int32)[None, :]
    flat_send = fine_send.reshape(-1)
    listed = jnp.clip((neighbour_device * 2 + row) * FB + fine_nbr, 0, N_GX * 2 * FB - 1).astype(jnp.int32)
    valid = (fine_nbr >= 0) & ((tap_x[None, :] == 0) | (flat_send[listed] == fine_nbr))
    src_fine = jnp.where(valid, target, NF).astype(jnp.int32)

    enc_fine = layer(features, src_fine, enc_fine_w, FB)
    pooled = enc_fine.astype(jnp.float32).reshape(NF, half, 2, half, 2, half, 2, width).mean(axis=(2, 4, 6))
    pooled = pooled.astype(jnp.bfloat16)
    pooled_table = jnp.concatenate([pooled, jnp.zeros((1, half, half, half, width), jnp.bfloat16)], axis=0)
    child_index = jnp.where(coarse_child >= 0, coarse_child, NF).astype(jnp.int32)
    coarse_in = from_octants(pooled_table[child_index], half)

    src_coarse = jnp.where(coarse_nbr >= 0, coarse_nbr, NC).astype(jnp.int32)
    enc_coarse = layer(coarse_in, src_coarse, enc_coarse_w, CB)
    dec_coarse = layer(enc_coarse, src_coarse, dec_coarse_w, CB)

    octants = to_octants(dec_coarse, half)
    octant_table = jnp.concatenate([octants, jnp.zeros((1, half, half, half, width), jnp.bfloat16)], axis=0)
    parent_index = jnp.where(fine_parent >= 0, fine_parent, NC * 8).astype(jnp.int32)
    upsampled = octant_table[parent_index]
    upsampled = jnp.repeat(jnp.repeat(jnp.repeat(upsampled, 2, axis=1), 2, axis=2), 2, axis=3)
    dec_in = (enc_fine.astype(jnp.float32) + upsampled.astype(jnp.float32)).astype(jnp.bfloat16)
    return layer(dec_in, src_fine, dec_fine_w, FB)
```

```python
import functools

import jax
import jax.numpy as jnp
from jax import lax
from jax.experimental import pallas as pl
from jax.experimental.pallas import tpu as pltpu
from jax.sharding import PartitionSpec as P

F32 = jnp.float32
BF16 = jnp.bfloat16
LANES = 4
MESH = pl.DeviceIdType.MESH


def pick(offset, edge):
    if offset < 0:
        return slice(edge - 1, edge)
    if offset == 0:
        return slice(0, edge)
    return slice(0, 1)


def place(offset, edge, base):
    if offset < 0:
        return slice(base - 1, base)
    if offset == 0:
        return slice(base, base + edge)
    return slice(base + edge, base + edge + 1)


def kernel(
    n,
    fine_nbr,
    fine_send,
    fine_parent,
    child_ref,
    nbr_ref,
    feat_hbm,
    w1_hbm,
    w2_hbm,
    w3_hbm,
    w4_hbm,
    out_ref,
    feat,
    w1,
    w2,
    w3,
    w4,
    pad,
    cols,
    table,
    enc,
    below,
    above,
    face_out,
    face_in,
    face_out2,
    face_in2,
    half_z,
    pooled,
    children,
    meta,
    meta_s,
    coarse,
    coarse2,
    coarse3,
    low_x,
    high_x,
    side_out,
    side_in,
    side_out2,
    side_in2,
    spread,
    lifted,
    load_sem,
    face_send_sem,
    face_recv_sem,
    pool_send_sem,
    pool_recv_sem,
    meta_send_sem,
    meta_recv_sem,
    side_send_sem,
    side_recv_sem,
    meta_sem,
):
    slots, edge = out_ref.shape[0], enc.shape[1]
    plane = edge * edge
    width = out_ref.shape[-1]
    half = edge // 2
    block = half**3
    per = child_ref.shape[0]
    bricks = LANES * per
    me = lax.axis_index("gx")
    member = lax.rem(me, LANES)
    group = lax.div(me, LANES)

    def peer(k):
        return me - member + (member ^ k)

    loads = [
        pltpu.make_async_copy(src, dst, load_sem.at[i])
        for i, (src, dst) in enumerate(
            ((feat_hbm, feat), (w1_hbm, w1), (w2_hbm, w2), (w3_hbm, w3), (w4_hbm, w4))
        )
    ]
    for copy in loads:
        copy.start()

    has_prev, has_next = me > 0, me < n - 1
    has_down, has_up = me >= LANES, me < n - LANES
    barrier = pltpu.get_barrier_semaphore()

    def greet(other):
        pl.semaphore_signal(barrier, inc=1, device_id={"gx": other}, device_id_type=MESH)

    sides = (
        (has_prev & (member == 0), me - 1),
        (has_next & (member == LANES - 1), me + 1),
        (has_down, me - LANES),
        (has_up, me + LANES),
    )
    for k in range(1, LANES):
        greet(peer(k))
    peers = LANES - 1
    for there, other in sides:
        pl.when(there)(functools.partial(greet, other))
        peers = peers + jnp.where(there, 1, 0)
    pl.semaphore_wait(barrier, peers)

    def remote(src, dst, send, recv, other):
        return pltpu.make_async_remote_copy(
            src_ref=src,
            dst_ref=dst,
            send_sem=send,
            recv_sem=recv,
            device_id={"gx": other},
            device_id_type=MESH,
        )

    def face_copies(outgoing, incoming, phase):
        up = remote(
            outgoing.at[0],
            incoming.at[0],
            face_send_sem.at[phase, 0],
            face_recv_sem.at[phase, 0],
            me + 1,
        )
        down = remote(
            outgoing.at[1],
            incoming.at[1],
            face_send_sem.at[phase, 1],
            face_recv_sem.at[phase, 1],
            me - 1,
        )
        return up, down

    def start_pair(up, up_there, down, down_there):
        pl.when(up_there)(up.start)
        pl.when(down_there)(down.start)

    def finish_pair(up, up_there, down, down_there):
        @pl.when(down_there)
        def _():
            up.wait_recv()
            down.wait_send()

        @pl.when(up_there)
        def _():
            down.wait_recv()
            up.wait_send()

    meta[member, 0:per, 0 : child_ref.shape[1]] = child_ref[...]
    meta[member, per : 2 * per, 0 : nbr_ref.shape[1]] = nbr_ref[...]

    cube = (edge, edge, edge, width)
    zero_brick = jnp.zeros(cube, F32)
    zero_plane = jnp.zeros((edge, edge, width), F32)
    table[slots] = zero_brick

    def stage_faces(outgoing, s):
        up_from = jnp.where(fine_send[0, s] >= 0, s, slots)
        down_from = jnp.where(fine_send[1, s] >= 0, s, slots)
        outgoing[0, s] = table[up_from, edge - 1].reshape(plane, width).astype(BF16)
        outgoing[1, s] = table[down_from, 0].reshape(plane, width).astype(BF16)

    loads[0].wait()
    for s in range(slots):
        table[s] = feat[s].astype(F32).reshape(cube)
    for s in range(slots):
        stage_faces(face_out, s)
    halo1 = face_copies(face_out, face_in, 0)
    start_pair(halo1[0], has_next, halo1[1], has_prev)
    meta_copies = [
        remote(
            meta.at[member],
            meta.at[member],
            meta_send_sem.at[k - 1],
            meta_recv_sem.at[k - 1],
            peer(k),
        )
        for k in range(1, LANES)
    ]
    for copy in meta_copies:
        copy.start()

    below[slots] = zero_plane
    above[slots] = zero_plane
    coarse[bricks] = zero_brick
    coarse2[bricks] = zero_brick
    coarse3[bricks] = zero_brick
    low_x[3 * bricks] = zero_plane
    high_x[3 * bricks] = zero_plane
    children[LANES * slots] = jnp.zeros((block, width), F32)

    base = edge

    def convolve(centre, lower, upper, index, weights):
        for t in range(27):
            dx, dy, dz = t // 9 - 1, t // 3 % 3 - 1, t % 3 - 1
            at = index(t)
            ys, zs = pick(dy, edge), pick(dz, edge)
            if dx == 0:
                piece = centre[at, :, ys, zs, :]
            elif dx < 0:
                piece = lower[at, ys, zs, :][None]
            else:
                piece = upper[at, ys, zs, :][None]
            pad[place(dx, edge, 1), place(dy, edge, 1), place(dz, edge, base), :] = piece
        for x in range(edge + 2):
            for k in range(9):
                dy, dz = k // 3, k % 3 - 1
                piece = pad[x, dy : dy + edge, base + dz : base + dz + edge, :]
                cols[x * plane : (x + 1) * plane, k * width : (k + 1) * width] = piece.reshape(
                    plane, width
                ).astype(BF16)
        total = None
        for dx in range(3):
            part = jnp.dot(
                cols[dx * plane : (dx + edge) * plane, :],
                weights[dx],
                preferred_element_type=F32,
            )
            total = part if total is None else total + part
        return jnp.maximum(total, 0.0).astype(BF16)

    def fine_index(b):
        def index(t):
            at = fine_nbr[b, t]
            return jnp.where(at >= 0, at, slots)

        return index

    def take_faces(incoming):
        for s in range(slots):
            below[s] = incoming[0, s].astype(F32).reshape(edge, edge, width)
            above[s] = incoming[1, s].astype(F32).reshape(edge, edge, width)

    finish_pair(halo1[0], has_next, halo1[1], has_prev)
    take_faces(face_in)
    loads[1].wait()

    def pool_copy(k, b):
        return remote(
            pooled.at[member, b],
            pooled.at[member, b],
            pool_send_sem.at[k - 1, b],
            pool_recv_sem.at[k - 1, b],
            peer(k),
        )

    @pl.loop(0, slots)
    def _(b):
        value = convolve(table, below, above, fine_index(b), w1).astype(F32).reshape(cube)
        enc[b] = value
        pairs = value.reshape(half, 2, half, 2, edge, width)
        summed = (pairs[:, 0, :, 0] + pairs[:, 0, :, 1]) + (pairs[:, 1, :, 0] + pairs[:, 1, :, 1])
        half_z[...] = summed.reshape(half * half * edge, width)
        even = half_z[pl.ds(0, block, stride=2), :]
        odd = half_z[pl.ds(1, block, stride=2), :]
        pooled[member, b] = ((even + odd) * 0.125).astype(BF16)
        for k in range(1, LANES):
            pool_copy(k, b).start()

    for copy in meta_copies:
        copy.wait()
    to_smem = pltpu.make_async_copy(meta, meta_s, meta_sem)
    to_smem.start()
    for k in range(1, LANES):
        for b in range(slots):
            pool_copy(k, b).wait()
    to_smem.wait()
    for lane in range(LANES):
        for s in range(slots):
            children[lane * slots + s] = pooled[lane, s].astype(F32)

    def owner_of(value):
        value = jnp.maximum(value, 0)
        return lax.div(value, per), lax.rem(value, per)

    @pl.loop(0, bricks)
    def _(j):
        lane, slot = lax.div(j, per), lax.rem(j, per)
        for o in range(8):
            child = meta_s[lane, slot, o]
            safe = jnp.maximum(child, 0)
            at = lax.rem(lax.div(safe, slots), LANES) * slots + lax.rem(safe, slots)
            at = jnp.where(child >= 0, at, LANES * slots)
            ox, oy, oz = o // 4 * half, o // 2 % 2 * half, o % 2 * half
            for x in range(half):
                for y in range(half):
                    row = (x * half + y) * half
                    coarse[j, ox + x, oy + y, oz : oz + half, :] = children[
                        at, row : row + half, :
                    ]

    def side_copies(outgoing, incoming, phase):
        up = remote(
            outgoing,
            incoming.at[0],
            side_send_sem.at[phase, 0],
            side_recv_sem.at[phase, 0],
            me + LANES,
        )
        down = remote(
            outgoing,
            incoming.at[1],
            side_send_sem.at[phase, 1],
            side_recv_sem.at[phase, 1],
            me - LANES,
        )
        return up, down

    def coarse_index(j):
        lane, slot = lax.div(j, per), lax.rem(j, per)

        def index(t):
            value = meta_s[lane, per + slot, t]
            device, at = owner_of(value)
            at = lax.rem(device, LANES) * per + at
            if t // 9 == 1:
                return jnp.where(value >= 0, at, bricks)
            at = at + (lax.div(device, LANES) - group + 1) * bricks
            at = jnp.minimum(jnp.maximum(at, 0), 3 * bricks)
            return jnp.where(value >= 0, at, 3 * bricks)

        return index

    def coarse_layer(source, target, outgoing, incoming, phase, weights):
        for j in range(bricks):
            first, last = source[j, 0], source[j, edge - 1]
            low_x[bricks + j] = first
            high_x[bricks + j] = last
            outgoing[j, 0] = first.reshape(plane, width).astype(BF16)
            outgoing[j, 1] = last.reshape(plane, width).astype(BF16)
        up, down = side_copies(outgoing, incoming, phase)
        start_pair(up, has_up, down, has_down)
        finish_pair(up, has_up, down, has_down)
        for side, start in ((0, 0), (1, 2 * bricks)):
            for j in range(bricks):
                low_x[start + j] = incoming[side, j, 0].astype(F32).reshape(edge, edge, width)
                high_x[start + j] = incoming[side, j, 1].astype(F32).reshape(edge, edge, width)

        @pl.loop(0, bricks)
        def _(j):
            value = convolve(source, high_x, low_x, coarse_index(j), weights)
            target[j] = value.astype(F32).reshape(cube)

    loads[2].wait()
    coarse_layer(coarse, coarse2, side_out, side_in, 0, w2)
    loads[3].wait()
    coarse_layer(coarse2, coarse3, side_out2, side_in2, 1, w3)

    for s in range(slots):
        parent = fine_parent[s]
        safe = jnp.maximum(parent, 0)
        device, at = owner_of(lax.div(safe, 8))
        at = jnp.where(parent >= 0, lax.rem(device, LANES) * per + at, bricks)
        octant = lax.rem(safe, 8)
        ox = lax.div(octant, 4)
        oy = lax.rem(lax.div(octant, 2), 2)
        oz = lax.rem(octant, 2)
        piece = coarse3[at, pl.ds(ox * half, half), pl.ds(oy * half, half), :, :]
        piece = piece.reshape(half * half * edge, width)
        spread[pl.ds(0, half * half * edge, stride=2), :] = piece
        spread[pl.ds(1, half * half * edge, stride=2), :] = piece
        for z in range(2):
            for row in range(half * half):
                start = row * 2 * edge + z * edge
                lifted[z, row] = spread[start : start + edge, :]
        for x in range(half):
            for y in range(half):
                up = lifted[oz, x * half + y]
                for xx in range(2):
                    for yy in range(2):
                        value = enc[s, 2 * x + xx, 2 * y + yy] + up
                        table[s, 2 * x + xx, 2 * y + yy] = value.astype(BF16).astype(F32)
        stage_faces(face_out2, s)
    halo2 = face_copies(face_out2, face_in2, 1)
    start_pair(halo2[0], has_next, halo2[1], has_prev)
    loads[4].wait()
    finish_pair(halo2[0], has_next, halo2[1], has_prev)
    take_faces(face_in2)

    @pl.loop(0, slots)
    def _(b):
        out_ref[b] = convolve(table, below, above, fine_index(b), w4)


def per_device(
    n,
    features,
    fine_nbr,
    fine_send,
    fine_parent,
    coarse_child,
    coarse_nbr,
    enc_fine_w,
    enc_coarse_w,
    dec_coarse_w,
    dec_fine_w,
):
    slots, edge, width = features.shape[0], features.shape[1], features.shape[-1]
    per = coarse_nbr.shape[0]
    bricks = LANES * per
    half = edge // 2
    plane = edge * edge
    voxels = edge**3
    rows = -(-2 * per // 8) * 8
    kernels = [
        w.reshape(3, 9 * width, width)
        for w in (enc_fine_w, enc_coarse_w, dec_coarse_w, dec_fine_w)
    ]
    vmem = pltpu.VMEM
    smem_spec = pl.BlockSpec(memory_space=pltpu.SMEM)
    vmem_spec = pl.BlockSpec(memory_space=pltpu.VMEM)
    any_spec = pl.BlockSpec(memory_space=pl.ANY)
    cube = (edge, edge, edge, width)
    face = (edge, edge, width)
    dma = pltpu.SemaphoreType.DMA
    out = pl.pallas_call(
        functools.partial(kernel, n),
        out_shape=jax.ShapeDtypeStruct((slots, voxels, width), BF16),
        in_specs=[smem_spec] * 3 + [vmem_spec] * 2 + [any_spec] * 5,
        out_specs=vmem_spec,
        scratch_shapes=[
            vmem((slots, voxels, width), BF16),
            *[vmem((3, 9 * width, width), BF16)] * 4,
            vmem((edge + 2, edge + 2, 3 * edge, width), F32),
            vmem(((edge + 2) * plane, 9 * width), BF16),
            vmem((slots + 1,) + cube, F32),
            vmem((slots,) + cube, F32),
            vmem((slots + 1,) + face, F32),
            vmem((slots + 1,) + face, F32),
            vmem((2, slots, plane, width), BF16),
            vmem((2, slots, plane, width), BF16),
            vmem((2, slots, plane, width), BF16),
            vmem((2, slots, plane, width), BF16),
            vmem((half * half * edge, width), F32),
            vmem((LANES, slots, half**3, width), BF16),
            vmem((LANES * slots + 1, half**3, width), F32),
            vmem((LANES, rows, 128), jnp.int32),
            pltpu.SMEM((LANES, rows, 128), jnp.int32),
            vmem((bricks + 1,) + cube, F32),
            vmem((bricks + 1,) + cube, F32),
            vmem((bricks + 1,) + cube, F32),
            vmem((3 * bricks + 1,) + face, F32),
            vmem((3 * bricks + 1,) + face, F32),
            vmem((bricks, 2, plane, width), BF16),
            vmem((2, bricks, 2, plane, width), BF16),
            vmem((bricks, 2, plane, width), BF16),
            vmem((2, bricks, 2, plane, width), BF16),
            vmem((half * half * 2 * edge, width), F32),
            vmem((2, half * half, edge, width), F32),
            dma((5,)),
            dma((2, 2)),
            dma((2, 2)),
            dma((LANES - 1, slots)),
            dma((LANES - 1, slots)),
            dma((LANES - 1,)),
            dma((LANES - 1,)),
            dma((2, 2)),
            dma((2, 2)),
            dma(()),
        ],
        compiler_params=pltpu.CompilerParams(
            collective_id=0, has_side_effects=True, vmem_limit_bytes=60 * 1024 * 1024
        ),
    )(
        fine_nbr,
        fine_send[0],
        fine_parent,
        coarse_child,
        coarse_nbr,
        features.reshape(slots, voxels, width),
        *kernels,
    )
    return out.reshape(features.shape)


def solution(mesh):
    lead = ("groups", "gx")
    placed = (
        P(lead, None, None, None, None),
        P(lead, None),
        P(lead, None, None),
        P(lead),
        P(lead, None),
        P(lead, None),
        P(),
        P(),
        P(),
        P(),
    )
    return jax.shard_map(
        functools.partial(per_device, mesh.shape["gx"]),
        mesh=mesh,
        in_specs=placed,
        out_specs=P(lead, None, None, None, None),
        check_vma=False,
    )
```

```python
import functools

import jax
import jax.numpy as jnp
from jax import lax
from jax.experimental import pallas as pl
from jax.experimental.pallas import tpu as pltpu
from jax.sharding import PartitionSpec as P

F32 = jnp.float32
BF16 = jnp.bfloat16
LANES = 4
MESH = pl.DeviceIdType.MESH


def pick(offset, edge):
    if offset < 0:
        return slice(edge - 1, edge)
    if offset == 0:
        return slice(0, edge)
    return slice(0, 1)


def place(offset, edge, base):
    if offset < 0:
        return slice(base - 1, base)
    if offset == 0:
        return slice(base, base + edge)
    return slice(base + edge, base + edge + 1)


def kernel(
    n,
    fine_nbr,
    fine_send,
    fine_parent,
    child_ref,
    nbr_ref,
    feat_hbm,
    w1_hbm,
    w2_hbm,
    w3_hbm,
    w4_hbm,
    out_ref,
    feat,
    w1,
    w2,
    w3,
    w4,
    pad,
    cols,
    table,
    enc,
    below,
    above,
    face_out,
    face_in,
    face_out2,
    face_in2,
    half_z,
    pooled,
    children,
    meta,
    meta_s,
    coarse,
    coarse2,
    low_x,
    high_x,
    side_out,
    side_in,
    side_out2,
    side_in2,
    spread,
    lifted,
    load_sem,
    face_send_sem,
    face_recv_sem,
    pool_send_sem,
    pool_recv_sem,
    meta_send_sem,
    meta_recv_sem,
    side_send_sem,
    side_recv_sem,
    meta_sem,
):
    slots, edge = out_ref.shape[0], enc.shape[1]
    plane = edge * edge
    width = out_ref.shape[-1]
    half = edge // 2
    block = half**3
    per = child_ref.shape[0]
    bricks = LANES * per
    me = lax.axis_index("gx")
    member = lax.rem(me, LANES)
    group = lax.div(me, LANES)

    def peer(k):
        return me - member + (member ^ k)

    width = out_ref.shape[-1]
    loads = [[pltpu.make_async_copy(feat_hbm, feat, load_sem.at[0, 0])]]
    for i, (src, dst) in enumerate(
        ((w1_hbm, w1), (w2_hbm, w2), (w3_hbm, w3), (w4_hbm, w4))
    ):
        loads.append(
            [
                pltpu.make_async_copy(
                    src.at[dx], dst.at[:, dx * width : (dx + 1) * width], load_sem.at[i + 1, dx]
                )
                for dx in range(3)
            ]
        )
    for copies in loads:
        for copy in copies:
            copy.start()

    def loaded(i):
        for copy in loads[i]:
            copy.wait()

    has_prev, has_next = me > 0, me < n - 1
    has_down, has_up = me >= LANES, me < n - LANES
    barrier = pltpu.get_barrier_semaphore()

    def greet(other):
        pl.semaphore_signal(barrier, inc=1, device_id={"gx": other}, device_id_type=MESH)

    sides = (
        (has_prev & (member == 0), me - 1),
        (has_next & (member == LANES - 1), me + 1),
        (has_down, me - LANES),
        (has_up, me + LANES),
    )
    for k in range(1, LANES):
        greet(peer(k))
    peers = LANES - 1
    for there, other in sides:
        pl.when(there)(functools.partial(greet, other))
        peers = peers + jnp.where(there, 1, 0)
    pl.semaphore_wait(barrier, peers)

    def remote(src, dst, send, recv, other):
        return pltpu.make_async_remote_copy(
            src_ref=src,
            dst_ref=dst,
            send_sem=send,
            recv_sem=recv,
            device_id={"gx": other},
            device_id_type=MESH,
        )

    def face_copies(outgoing, incoming, phase):
        up = remote(
            outgoing.at[0],
            incoming.at[0],
            face_send_sem.at[phase, 0],
            face_recv_sem.at[phase, 0],
            me + 1,
        )
        down = remote(
            outgoing.at[1],
            incoming.at[1],
            face_send_sem.at[phase, 1],
            face_recv_sem.at[phase, 1],
            me - 1,
        )
        return up, down

    def start_pair(up, up_there, down, down_there):
        pl.when(up_there)(up.start)
        pl.when(down_there)(down.start)

    def finish_pair(up, up_there, down, down_there):
        @pl.when(down_there)
        def _():
            up.wait_recv()
            down.wait_send()

        @pl.when(up_there)
        def _():
            down.wait_recv()
            up.wait_send()

    meta[member, 0:per, 0 : child_ref.shape[1]] = child_ref[...]
    meta[member, per : 2 * per, 0 : nbr_ref.shape[1]] = nbr_ref[...]

    cube = (edge, edge, edge, width)
    zero_brick = jnp.zeros(cube, F32)
    zero_plane = jnp.zeros((edge, edge, width), F32)
    table[slots] = zero_brick

    def stage_faces(outgoing, s):
        up_from = jnp.where(fine_send[0, s] >= 0, s, slots)
        down_from = jnp.where(fine_send[1, s] >= 0, s, slots)
        outgoing[0, s] = table[up_from, edge - 1].reshape(plane, width).astype(BF16)
        outgoing[1, s] = table[down_from, 0].reshape(plane, width).astype(BF16)

    loaded(0)
    for s in range(slots):
        table[s] = feat[s].astype(F32).reshape(cube)
    for s in range(slots):
        stage_faces(face_out, s)
    halo1 = face_copies(face_out, face_in, 0)
    start_pair(halo1[0], has_next, halo1[1], has_prev)
    meta_copies = [
        remote(
            meta.at[member],
            meta.at[member],
            meta_send_sem.at[k - 1],
            meta_recv_sem.at[k - 1],
            peer(k),
        )
        for k in range(1, LANES)
    ]
    for copy in meta_copies:
        copy.start()

    below[slots] = zero_plane
    above[slots] = zero_plane
    coarse[bricks] = zero_brick
    coarse2[bricks] = zero_brick
    low_x[3 * bricks] = zero_plane
    high_x[3 * bricks] = zero_plane
    children[LANES * slots] = jnp.zeros((block, width), F32)

    base = edge

    def assemble(centre, lower, upper, index):
        for t in range(27):
            dx, dy, dz = t // 9 - 1, t // 3 % 3 - 1, t % 3 - 1
            at = index(t)
            ys, zs = pick(dy, edge), pick(dz, edge)
            if dx == 0:
                piece = centre[at, :, ys, zs, :]
            elif dx < 0:
                piece = lower[at, ys, zs, :][None]
            else:
                piece = upper[at, ys, zs, :][None]
            pad[place(dx, edge, 1), place(dy, edge, 1), place(dz, edge, base), :] = piece

    def product(weights, planes, rows):
        two = jnp.dot(
            cols[0 : (planes + 1) * rows, :],
            weights[:, 0 : 2 * width],
            preferred_element_type=F32,
        )
        third = jnp.dot(
            cols[2 * rows : (planes + 2) * rows, :],
            weights[:, 2 * width : 3 * width],
            preferred_element_type=F32,
        )
        total = third + two[0 : planes * rows, 0:width] + two[rows:, width : 2 * width]
        return jnp.maximum(total, 0.0).astype(BF16)

    def convolve(centre, lower, upper, index, weights):
        assemble(centre, lower, upper, index)
        for x in range(edge + 2):
            for k in range(9):
                dy, dz = k // 3, k % 3 - 1
                piece = pad[x, dy : dy + edge, base + dz : base + dz + edge, :]
                cols[x * plane : (x + 1) * plane, k * width : (k + 1) * width] = piece.reshape(
                    plane, width
                ).astype(BF16)
        return product(weights, edge, plane)

    def fine_index(b):
        def index(t):
            at = fine_nbr[b, t]
            return jnp.where(at >= 0, at, slots)

        return index

    def take_faces(incoming):
        for s in range(slots):
            below[s] = incoming[0, s].astype(F32).reshape(edge, edge, width)
            above[s] = incoming[1, s].astype(F32).reshape(edge, edge, width)

    finish_pair(halo1[0], has_next, halo1[1], has_prev)
    take_faces(face_in)
    loaded(1)

    def pool_copy(k, b):
        return remote(
            pooled.at[member, b],
            pooled.at[member, b],
            pool_send_sem.at[k - 1, b],
            pool_recv_sem.at[k - 1, b],
            peer(k),
        )

    @pl.loop(0, slots)
    def _(b):
        value = convolve(table, below, above, fine_index(b), w1).astype(F32).reshape(cube)
        enc[b] = value
        pairs = value.reshape(half, 2, half, 2, edge, width)
        summed = (pairs[:, 0, :, 0] + pairs[:, 0, :, 1]) + (pairs[:, 1, :, 0] + pairs[:, 1, :, 1])
        half_z[...] = summed.reshape(half * half * edge, width)
        even = half_z[pl.ds(0, block, stride=2), :]
        odd = half_z[pl.ds(1, block, stride=2), :]
        pooled[member, b] = ((even + odd) * 0.125).astype(BF16)
        for k in range(1, LANES):
            pool_copy(k, b).start()

    for copy in meta_copies:
        copy.wait()
    to_smem = pltpu.make_async_copy(meta, meta_s, meta_sem)
    to_smem.start()
    for k in range(1, LANES):
        for b in range(slots):
            pool_copy(k, b).wait()
    to_smem.wait()
    for lane in range(LANES):
        for s in range(slots):
            children[lane * slots + s] = pooled[lane, s].astype(F32)

    def owner_of(value):
        value = jnp.maximum(value, 0)
        return lax.div(value, per), lax.rem(value, per)

    @pl.loop(0, bricks)
    def _(j):
        lane, slot = lax.div(j, per), lax.rem(j, per)
        for o in range(8):
            child = meta_s[lane, slot, o]
            safe = jnp.maximum(child, 0)
            at = lax.rem(lax.div(safe, slots), LANES) * slots + lax.rem(safe, slots)
            at = jnp.where(child >= 0, at, LANES * slots)
            ox, oy, oz = o // 4 * half, o // 2 % 2 * half, o % 2 * half
            for x in range(half):
                for y in range(half):
                    row = (x * half + y) * half
                    coarse[j, ox + x, oy + y, oz : oz + half, :] = children[
                        at, row : row + half, :
                    ]

    def side_copies(outgoing, incoming, phase):
        up = remote(
            outgoing,
            incoming.at[0],
            side_send_sem.at[phase, 0],
            side_recv_sem.at[phase, 0],
            me + LANES,
        )
        down = remote(
            outgoing,
            incoming.at[1],
            side_send_sem.at[phase, 1],
            side_recv_sem.at[phase, 1],
            me - LANES,
        )
        return up, down

    def coarse_index(lane, slot, live):
        def index(t):
            value = meta_s[lane, per + slot, t]
            there = (value >= 0) & live
            device, at = owner_of(value)
            at = lax.rem(device, LANES) * per + at
            if t // 9 == 1:
                return jnp.where(there, at, bricks)
            at = at + (lax.div(device, LANES) - group + 1) * bricks
            at = jnp.minimum(jnp.maximum(at, 0), 3 * bricks)
            return jnp.where(there, at, 3 * bricks)

        return index

    def exchange_sides(source, outgoing, incoming, phase):
        for j in range(bricks):
            first, last = source[j, 0], source[j, edge - 1]
            low_x[bricks + j] = first
            high_x[bricks + j] = last
            outgoing[j, 0] = first.reshape(plane, width).astype(BF16)
            outgoing[j, 1] = last.reshape(plane, width).astype(BF16)
        up, down = side_copies(outgoing, incoming, phase)
        start_pair(up, has_up, down, has_down)
        finish_pair(up, has_up, down, has_down)
        for side, start in ((0, 0), (1, 2 * bricks)):
            for j in range(bricks):
                low_x[start + j] = incoming[side, j, 0].astype(F32).reshape(edge, edge, width)
                high_x[start + j] = incoming[side, j, 1].astype(F32).reshape(edge, edge, width)

    exchange_sides(coarse, side_out, side_in, 0)
    loaded(2)

    @pl.loop(0, bricks)
    def _(j):
        lane, slot = lax.div(j, per), lax.rem(j, per)
        value = convolve(coarse, high_x, low_x, coarse_index(lane, slot, True), w2)
        coarse2[j] = value.astype(F32).reshape(cube)

    exchange_sides(coarse2, side_out2, side_in2, 1)
    loaded(3)

    part = half * edge
    strip = slots * part

    @pl.loop(0, slots)
    def _(s):
        parent = fine_parent[s]
        safe = jnp.maximum(parent, 0)
        device, slot = owner_of(lax.div(safe, 8))
        octant = lax.rem(safe, 8)
        ox = lax.div(octant, 4) * half
        oy = lax.rem(lax.div(octant, 2), 2) * half
        assemble(
            coarse2, high_x, low_x, coarse_index(lax.rem(device, LANES), slot, parent >= 0)
        )
        for x in range(half + 2):
            start = pl.multiple_of(x * strip + s * part, part)
            for k in range(9):
                dy, dz = k // 3, k % 3 - 1
                piece = pad[ox + x, pl.ds(oy + dy, half), base + dz : base + dz + edge, :]
                cols[pl.ds(start, part), k * width : (k + 1) * width] = piece.reshape(
                    part, width
                ).astype(BF16)

    parents = product(w3, half, strip).astype(F32).reshape(half, slots, part, width)

    for s in range(slots):
        oz = lax.rem(jnp.maximum(fine_parent[s], 0), 2)
        piece = parents[:, s].reshape(half * half * edge, width)
        spread[pl.ds(0, half * half * edge, stride=2), :] = piece
        spread[pl.ds(1, half * half * edge, stride=2), :] = piece
        for z in range(2):
            for row in range(half * half):
                start = row * 2 * edge + z * edge
                lifted[z, row] = spread[start : start + edge, :]
        for x in range(half):
            for y in range(half):
                up = lifted[oz, x * half + y]
                for xx in range(2):
                    for yy in range(2):
                        value = enc[s, 2 * x + xx, 2 * y + yy] + up
                        table[s, 2 * x + xx, 2 * y + yy] = value.astype(BF16).astype(F32)
        stage_faces(face_out2, s)
    halo2 = face_copies(face_out2, face_in2, 1)
    start_pair(halo2[0], has_next, halo2[1], has_prev)
    loaded(4)
    finish_pair(halo2[0], has_next, halo2[1], has_prev)
    take_faces(face_in2)

    @pl.loop(0, slots)
    def _(b):
        out_ref[b] = convolve(table, below, above, fine_index(b), w4)


def per_device(
    n,
    features,
    fine_nbr,
    fine_send,
    fine_parent,
    coarse_child,
    coarse_nbr,
    enc_fine_w,
    enc_coarse_w,
    dec_coarse_w,
    dec_fine_w,
):
    slots, edge, width = features.shape[0], features.shape[1], features.shape[-1]
    per = coarse_nbr.shape[0]
    bricks = LANES * per
    half = edge // 2
    plane = edge * edge
    voxels = edge**3
    strip = slots * half * edge
    rows = -(-2 * per // 8) * 8
    kernels = [
        w.reshape(3, 9 * width, width)
        for w in (enc_fine_w, enc_coarse_w, dec_coarse_w, dec_fine_w)
    ]
    vmem = pltpu.VMEM
    smem_spec = pl.BlockSpec(memory_space=pltpu.SMEM)
    vmem_spec = pl.BlockSpec(memory_space=pltpu.VMEM)
    any_spec = pl.BlockSpec(memory_space=pl.ANY)
    cube = (edge, edge, edge, width)
    face = (edge, edge, width)
    dma = pltpu.SemaphoreType.DMA
    out = pl.pallas_call(
        functools.partial(kernel, n),
        out_shape=jax.ShapeDtypeStruct((slots, voxels, width), BF16),
        in_specs=[smem_spec] * 3 + [vmem_spec] * 2 + [any_spec] * 5,
        out_specs=vmem_spec,
        scratch_shapes=[
            vmem((slots, voxels, width), BF16),
            *[vmem((9 * width, 3 * width), BF16)] * 4,
            vmem((edge + 2, edge + 2, 3 * edge, width), F32),
            vmem((max((edge + 2) * plane, (half + 2) * strip), 9 * width), BF16),
            vmem((slots + 1,) + cube, F32),
            vmem((slots,) + cube, F32),
            vmem((slots + 1,) + face, F32),
            vmem((slots + 1,) + face, F32),
            vmem((2, slots, plane, width), BF16),
            vmem((2, slots, plane, width), BF16),
            vmem((2, slots, plane, width), BF16),
            vmem((2, slots, plane, width), BF16),
            vmem((half * half * edge, width), F32),
            vmem((LANES, slots, half**3, width), BF16),
            vmem((LANES * slots + 1, half**3, width), F32),
            vmem((LANES, rows, 128), jnp.int32),
            pltpu.SMEM((LANES, rows, 128), jnp.int32),
            vmem((bricks + 1,) + cube, F32),
            vmem((bricks + 1,) + cube, F32),
            vmem((3 * bricks + 1,) + face, F32),
            vmem((3 * bricks + 1,) + face, F32),
            vmem((bricks, 2, plane, width), BF16),
            vmem((2, bricks, 2, plane, width), BF16),
            vmem((bricks, 2, plane, width), BF16),
            vmem((2, bricks, 2, plane, width), BF16),
            vmem((half * half * 2 * edge, width), F32),
            vmem((2, half * half, edge, width), F32),
            dma((5, 3)),
            dma((2, 2)),
            dma((2, 2)),
            dma((LANES - 1, slots)),
            dma((LANES - 1, slots)),
            dma((LANES - 1,)),
            dma((LANES - 1,)),
            dma((2, 2)),
            dma((2, 2)),
            dma(()),
        ],
        compiler_params=pltpu.CompilerParams(
            collective_id=0, has_side_effects=True, vmem_limit_bytes=60 * 1024 * 1024
        ),
    )(
        fine_nbr,
        fine_send[0],
        fine_parent,
        coarse_child,
        coarse_nbr,
        features.reshape(slots, voxels, width),
        *kernels,
    )
    return out.reshape(features.shape)


def solution(mesh):
    lead = ("groups", "gx")
    placed = (
        P(lead, None, None, None, None),
        P(lead, None),
        P(lead, None, None),
        P(lead),
        P(lead, None),
        P(lead, None),
        P(),
        P(),
        P(),
        P(),
    )
    return jax.shard_map(
        functools.partial(per_device, mesh.shape["gx"]),
        mesh=mesh,
        in_specs=placed,
        out_specs=P(lead, None, None, None, None),
        check_vma=False,
    )
```

```python
import functools

import jax
import jax.numpy as jnp
from jax import lax
from jax.experimental import pallas as pl
from jax.experimental.pallas import tpu as pltpu
from jax.sharding import PartitionSpec as P

F32 = jnp.float32
BF16 = jnp.bfloat16
LANES = 4
MESH = pl.DeviceIdType.MESH


def pick(offset, edge):
    if offset < 0:
        return slice(edge - 1, edge)
    if offset == 0:
        return slice(0, edge)
    return slice(0, 1)


def place(offset, edge, base):
    if offset < 0:
        return slice(base - 1, base)
    if offset == 0:
        return slice(base, base + edge)
    return slice(base + edge, base + edge + 1)


def kernel(
    n,
    fine_nbr,
    fine_send,
    fine_parent,
    child_ref,
    nbr_ref,
    feat_hbm,
    w1_hbm,
    w2_hbm,
    w3_hbm,
    w4_hbm,
    out_ref,
    feat,
    w1,
    w2,
    w3,
    w4,
    pad,
    cols,
    opened,
    table,
    enc,
    below,
    above,
    face_out,
    face_in,
    face_out2,
    face_in2,
    half_z,
    pooled,
    children,
    meta,
    meta_s,
    coarse,
    coarse2,
    low_x,
    high_x,
    side_out,
    side_in,
    side_out2,
    side_in2,
    spread,
    lifted,
    load_sem,
    face_send_sem,
    face_recv_sem,
    pool_send_sem,
    pool_recv_sem,
    meta_send_sem,
    meta_recv_sem,
    side_send_sem,
    side_recv_sem,
    meta_sem,
):
    slots, edge = out_ref.shape[0], enc.shape[1]
    plane = edge * edge
    width = out_ref.shape[-1]
    half = edge // 2
    block = half**3
    per = child_ref.shape[0]
    bricks = LANES * per
    me = lax.axis_index("gx")
    member = lax.rem(me, LANES)
    group = lax.div(me, LANES)

    def peer(k):
        return me - member + (member ^ k)

    width = out_ref.shape[-1]
    loads = [[pltpu.make_async_copy(feat_hbm, feat, load_sem.at[0, 0])]]
    for i, (src, dst) in enumerate(
        ((w1_hbm, w1), (w2_hbm, w2), (w3_hbm, w3), (w4_hbm, w4))
    ):
        loads.append(
            [
                pltpu.make_async_copy(
                    src.at[dx], dst.at[:, dx * width : (dx + 1) * width], load_sem.at[i + 1, dx]
                )
                for dx in range(3)
            ]
        )
    for copies in loads:
        for copy in copies:
            copy.start()

    def loaded(i):
        for copy in loads[i]:
            copy.wait()

    has_prev, has_next = me > 0, me < n - 1
    has_down, has_up = me >= LANES, me < n - LANES
    barrier = pltpu.get_barrier_semaphore()

    def greet(other):
        pl.semaphore_signal(barrier, inc=1, device_id={"gx": other}, device_id_type=MESH)

    sides = (
        (has_prev & (member == 0), me - 1),
        (has_next & (member == LANES - 1), me + 1),
        (has_down, me - LANES),
        (has_up, me + LANES),
    )
    for k in range(1, LANES):
        greet(peer(k))
    peers = LANES - 1
    for there, other in sides:
        pl.when(there)(functools.partial(greet, other))
        peers = peers + jnp.where(there, 1, 0)
    pl.semaphore_wait(barrier, peers)

    def remote(src, dst, send, recv, other):
        return pltpu.make_async_remote_copy(
            src_ref=src,
            dst_ref=dst,
            send_sem=send,
            recv_sem=recv,
            device_id={"gx": other},
            device_id_type=MESH,
        )

    def face_copies(outgoing, incoming, phase):
        up = remote(
            outgoing.at[0],
            incoming.at[0],
            face_send_sem.at[phase, 0],
            face_recv_sem.at[phase, 0],
            me + 1,
        )
        down = remote(
            outgoing.at[1],
            incoming.at[1],
            face_send_sem.at[phase, 1],
            face_recv_sem.at[phase, 1],
            me - 1,
        )
        return up, down

    def start_pair(up, up_there, down, down_there):
        pl.when(up_there)(up.start)
        pl.when(down_there)(down.start)

    def finish_pair(up, up_there, down, down_there):
        @pl.when(down_there)
        def _():
            up.wait_recv()
            down.wait_send()

        @pl.when(up_there)
        def _():
            down.wait_recv()
            up.wait_send()

    meta[member, 0:per, 0 : child_ref.shape[1]] = child_ref[...]
    meta[member, per : 2 * per, 0 : nbr_ref.shape[1]] = nbr_ref[...]

    cube = (edge, edge, edge, width)
    zero_brick = jnp.zeros(cube, F32)
    zero_plane = jnp.zeros((edge, edge, width), F32)
    table[slots] = zero_brick

    def stage_faces(outgoing, s):
        up_from = jnp.where(fine_send[0, s] >= 0, s, slots)
        down_from = jnp.where(fine_send[1, s] >= 0, s, slots)
        outgoing[0, s] = table[up_from, edge - 1].reshape(plane, width).astype(BF16)
        outgoing[1, s] = table[down_from, 0].reshape(plane, width).astype(BF16)

    loaded(0)
    for s in range(slots):
        table[s] = feat[s].astype(F32).reshape(cube)
    for s in range(slots):
        stage_faces(face_out, s)
    halo1 = face_copies(face_out, face_in, 0)
    start_pair(halo1[0], has_next, halo1[1], has_prev)
    meta_copies = [
        remote(
            meta.at[member],
            meta.at[member],
            meta_send_sem.at[k - 1],
            meta_recv_sem.at[k - 1],
            peer(k),
        )
        for k in range(1, LANES)
    ]
    for copy in meta_copies:
        copy.start()

    below[slots] = zero_plane
    above[slots] = zero_plane
    coarse[bricks] = zero_brick
    coarse2[bricks] = zero_brick
    low_x[3 * bricks] = zero_plane
    high_x[3 * bricks] = zero_plane
    children[LANES * slots] = jnp.zeros((block, width), F32)

    base = edge

    def assemble(centre, lower, upper, index, taps=range(27)):
        for t in taps:
            dx, dy, dz = t // 9 - 1, t // 3 % 3 - 1, t % 3 - 1
            at = index(t)
            ys, zs = pick(dy, edge), pick(dz, edge)
            if dx == 0:
                piece = centre[at, :, ys, zs, :]
            elif dx < 0:
                piece = lower[at, ys, zs, :][None]
            else:
                piece = upper[at, ys, zs, :][None]
            pad[place(dx, edge, 1), place(dy, edge, 1), place(dz, edge, base), :] = piece

    def product(weights, planes, rows):
        two = jnp.dot(
            cols[0 : (planes + 1) * rows, :],
            weights[:, 0 : 2 * width],
            preferred_element_type=F32,
        )
        third = jnp.dot(
            cols[2 * rows : (planes + 2) * rows, :],
            weights[:, 2 * width : 3 * width],
            preferred_element_type=F32,
        )
        total = third + two[0 : planes * rows, 0:width] + two[rows:, width : 2 * width]
        return jnp.maximum(total, 0.0).astype(BF16)

    def convolve(centre, lower, upper, index, weights):
        assemble(centre, lower, upper, index)
        for x in range(edge + 2):
            for k in range(9):
                dy, dz = k // 3, k % 3 - 1
                piece = pad[x, dy : dy + edge, base + dz : base + dz + edge, :]
                cols[x * plane : (x + 1) * plane, k * width : (k + 1) * width] = piece.reshape(
                    plane, width
                ).astype(BF16)
        return product(weights, edge, plane)

    own_taps = range(9, 18)
    far_taps = (*range(9), *range(18, 27))

    def gather_columns(x, row):
        for k in range(9):
            dy, dz = k // 3, k % 3 - 1
            piece = pad[x, dy : dy + edge, base + dz : base + dz + edge, :]
            cols[pl.ds(row, plane), k * width : (k + 1) * width] = piece.reshape(
                plane, width
            ).astype(BF16)

    def local_product(centre, j, index, weights):
        assemble(centre, None, None, index, own_taps)
        for x in range(edge):
            gather_columns(x + 1, x * plane)
        two = jnp.dot(
            cols[0 : edge * plane, :], weights[:, 0 : 2 * width], preferred_element_type=F32
        )
        third = jnp.dot(
            cols[plane : edge * plane, :],
            weights[:, 2 * width : 3 * width],
            preferred_element_type=F32,
        )
        inner = slice(plane, (edge - 1) * plane)
        middle = two[:, width : 2 * width]
        opened[j, 0] = middle[0:plane] + third[0:plane]
        opened[j, 1] = middle[(edge - 1) * plane :] + two[(edge - 2) * plane : (edge - 1) * plane, 0:width]
        total = middle[inner] + third[inner] + two[0 : (edge - 2) * plane, 0:width]
        return jnp.maximum(total, 0.0).astype(BF16)

    def outer_planes(count, lower, upper, index_of, weights, store):
        @pl.loop(0, count)
        def _(j):
            assemble(None, lower, upper, index_of(j), far_taps)
            gather_columns(0, pl.multiple_of(j * plane, plane))
            gather_columns(edge + 1, pl.multiple_of((count + j) * plane, plane))

        for side in range(2):
            added = jnp.dot(
                cols[side * count * plane : (side + 1) * count * plane, :],
                weights[:, 2 * side * width : (2 * side + 1) * width],
                preferred_element_type=F32,
            )
            for j in range(count):
                total = opened[j, side] + added[j * plane : (j + 1) * plane]
                store(j, side * (edge - 1), jnp.maximum(total, 0.0).astype(BF16))

    def fine_index(b):
        def index(t):
            at = fine_nbr[b, t]
            return jnp.where(at >= 0, at, slots)

        return index

    def take_faces(incoming):
        for s in range(slots):
            below[s] = incoming[0, s].astype(F32).reshape(edge, edge, width)
            above[s] = incoming[1, s].astype(F32).reshape(edge, edge, width)

    finish_pair(halo1[0], has_next, halo1[1], has_prev)
    take_faces(face_in)
    loaded(1)

    def pool_copy(k, b):
        return remote(
            pooled.at[member, b],
            pooled.at[member, b],
            pool_send_sem.at[k - 1, b],
            pool_recv_sem.at[k - 1, b],
            peer(k),
        )

    @pl.loop(0, slots)
    def _(b):
        value = convolve(table, below, above, fine_index(b), w1).astype(F32).reshape(cube)
        enc[b] = value
        pairs = value.reshape(half, 2, half, 2, edge, width)
        summed = (pairs[:, 0, :, 0] + pairs[:, 0, :, 1]) + (pairs[:, 1, :, 0] + pairs[:, 1, :, 1])
        half_z[...] = summed.reshape(half * half * edge, width)
        even = half_z[pl.ds(0, block, stride=2), :]
        odd = half_z[pl.ds(1, block, stride=2), :]
        pooled[member, b] = ((even + odd) * 0.125).astype(BF16)
        for k in range(1, LANES):
            pool_copy(k, b).start()

    for copy in meta_copies:
        copy.wait()
    to_smem = pltpu.make_async_copy(meta, meta_s, meta_sem)
    to_smem.start()
    for k in range(1, LANES):
        for b in range(slots):
            pool_copy(k, b).wait()
    to_smem.wait()
    for lane in range(LANES):
        for s in range(slots):
            children[lane * slots + s] = pooled[lane, s].astype(F32)

    def owner_of(value):
        value = jnp.maximum(value, 0)
        return lax.div(value, per), lax.rem(value, per)

    @pl.loop(0, bricks)
    def _(j):
        lane, slot = lax.div(j, per), lax.rem(j, per)
        for o in range(8):
            child = meta_s[lane, slot, o]
            safe = jnp.maximum(child, 0)
            at = lax.rem(lax.div(safe, slots), LANES) * slots + lax.rem(safe, slots)
            at = jnp.where(child >= 0, at, LANES * slots)
            ox, oy, oz = o // 4 * half, o // 2 % 2 * half, o % 2 * half
            for x in range(half):
                for y in range(half):
                    row = (x * half + y) * half
                    coarse[j, ox + x, oy + y, oz : oz + half, :] = children[
                        at, row : row + half, :
                    ]

    def side_copies(outgoing, incoming, phase):
        up = remote(
            outgoing,
            incoming.at[0],
            side_send_sem.at[phase, 0],
            side_recv_sem.at[phase, 0],
            me + LANES,
        )
        down = remote(
            outgoing,
            incoming.at[1],
            side_send_sem.at[phase, 1],
            side_recv_sem.at[phase, 1],
            me - LANES,
        )
        return up, down

    def coarse_index(lane, slot, live):
        def index(t):
            value = meta_s[lane, per + slot, t]
            there = (value >= 0) & live
            device, at = owner_of(value)
            at = lax.rem(device, LANES) * per + at
            if t // 9 == 1:
                return jnp.where(there, at, bricks)
            at = at + (lax.div(device, LANES) - group + 1) * bricks
            at = jnp.minimum(jnp.maximum(at, 0), 3 * bricks)
            return jnp.where(there, at, 3 * bricks)

        return index

    def send_sides(source, outgoing, incoming, phase):
        for j in range(bricks):
            first, last = source[j, 0], source[j, edge - 1]
            low_x[bricks + j] = first
            high_x[bricks + j] = last
            outgoing[j, 0] = first.reshape(plane, width).astype(BF16)
            outgoing[j, 1] = last.reshape(plane, width).astype(BF16)
        up, down = side_copies(outgoing, incoming, phase)
        start_pair(up, has_up, down, has_down)
        return up, down

    def take_sides(copies, incoming):
        finish_pair(copies[0], has_up, copies[1], has_down)
        for side, start in ((0, 0), (1, 2 * bricks)):
            for j in range(bricks):
                low_x[start + j] = incoming[side, j, 0].astype(F32).reshape(edge, edge, width)
                high_x[start + j] = incoming[side, j, 1].astype(F32).reshape(edge, edge, width)

    def group_index(j):
        return coarse_index(lax.div(j, per), lax.rem(j, per), True)

    face = (edge, edge, width)
    copies = send_sides(coarse, side_out, side_in, 0)
    loaded(2)

    @pl.loop(0, bricks)
    def _(j):
        value = local_product(coarse, j, group_index(j), w2).astype(F32)
        coarse2[j, 1 : edge - 1] = value.reshape((edge - 2,) + face)

    take_sides(copies, side_in)

    def store_coarse(j, x, value):
        coarse2[j, x] = value.astype(F32).reshape(face)

    outer_planes(bricks, high_x, low_x, group_index, w2, store_coarse)
    copies = send_sides(coarse2, side_out2, side_in2, 1)
    loaded(3)

    part = half * edge
    strip = slots * part

    def quarter(s, taps, planes):
        parent = fine_parent[s]
        safe = jnp.maximum(parent, 0)
        device, slot = owner_of(lax.div(safe, 8))
        octant = lax.rem(safe, 8)
        ox = lax.div(octant, 4) * half
        oy = lax.rem(lax.div(octant, 2), 2) * half
        index = coarse_index(lax.rem(device, LANES), slot, parent >= 0)
        assemble(coarse2, high_x, low_x, index, taps)
        for x in planes:
            start = pl.multiple_of(x * strip + s * part, part)
            for k in range(9):
                dy, dz = k // 3, k % 3 - 1
                piece = pad[ox + x, pl.ds(oy + dy, half), base + dz : base + dz + edge, :]
                cols[pl.ds(start, part), k * width : (k + 1) * width] = piece.reshape(
                    part, width
                ).astype(BF16)

    @pl.loop(0, slots)
    def _(s):
        quarter(s, own_taps, range(1, half + 1))

    take_sides(copies, side_in2)

    @pl.loop(0, slots)
    def _(s):
        quarter(s, range(27), (0, half + 1))

    parents = product(w3, half, strip).astype(F32).reshape(half, slots, part, width)

    for s in range(slots):
        oz = lax.rem(jnp.maximum(fine_parent[s], 0), 2)
        piece = parents[:, s].reshape(half * half * edge, width)
        spread[pl.ds(0, half * half * edge, stride=2), :] = piece
        spread[pl.ds(1, half * half * edge, stride=2), :] = piece
        for z in range(2):
            for row in range(half * half):
                start = row * 2 * edge + z * edge
                lifted[z, row] = spread[start : start + edge, :]
        for x in range(half):
            for y in range(half):
                up = lifted[oz, x * half + y]
                for xx in range(2):
                    for yy in range(2):
                        value = enc[s, 2 * x + xx, 2 * y + yy] + up
                        table[s, 2 * x + xx, 2 * y + yy] = value.astype(BF16).astype(F32)
        stage_faces(face_out2, s)
    halo2 = face_copies(face_out2, face_in2, 1)
    start_pair(halo2[0], has_next, halo2[1], has_prev)
    loaded(4)

    @pl.loop(0, slots)
    def _(b):
        value = local_product(table, b, fine_index(b), w4)
        out_ref[b, plane : (edge - 1) * plane, :] = value

    finish_pair(halo2[0], has_next, halo2[1], has_prev)
    take_faces(face_in2)

    def store_fine(b, x, value):
        out_ref[b, x * plane : (x + 1) * plane, :] = value

    outer_planes(slots, below, above, fine_index, w4, store_fine)


def per_device(
    n,
    features,
    fine_nbr,
    fine_send,
    fine_parent,
    coarse_child,
    coarse_nbr,
    enc_fine_w,
    enc_coarse_w,
    dec_coarse_w,
    dec_fine_w,
):
    slots, edge, width = features.shape[0], features.shape[1], features.shape[-1]
    per = coarse_nbr.shape[0]
    bricks = LANES * per
    half = edge // 2
    plane = edge * edge
    voxels = edge**3
    strip = slots * half * edge
    rows = -(-2 * per // 8) * 8
    kernels = [
        w.reshape(3, 9 * width, width)
        for w in (enc_fine_w, enc_coarse_w, dec_coarse_w, dec_fine_w)
    ]
    vmem = pltpu.VMEM
    smem_spec = pl.BlockSpec(memory_space=pltpu.SMEM)
    vmem_spec = pl.BlockSpec(memory_space=pltpu.VMEM)
    any_spec = pl.BlockSpec(memory_space=pl.ANY)
    cube = (edge, edge, edge, width)
    face = (edge, edge, width)
    dma = pltpu.SemaphoreType.DMA
    out = pl.pallas_call(
        functools.partial(kernel, n),
        out_shape=jax.ShapeDtypeStruct((slots, voxels, width), BF16),
        in_specs=[smem_spec] * 3 + [vmem_spec] * 2 + [any_spec] * 5,
        out_specs=vmem_spec,
        scratch_shapes=[
            vmem((slots, voxels, width), BF16),
            *[vmem((9 * width, 3 * width), BF16)] * 4,
            vmem((edge + 2, edge + 2, 3 * edge, width), F32),
            vmem((max((edge + 2) * plane, (half + 2) * strip, 2 * max(slots, bricks) * plane), 9 * width), BF16),
            vmem((max(slots, bricks), 2, plane, width), F32),
            vmem((slots + 1,) + cube, F32),
            vmem((slots,) + cube, F32),
            vmem((slots + 1,) + face, F32),
            vmem((slots + 1,) + face, F32),
            vmem((2, slots, plane, width), BF16),
            vmem((2, slots, plane, width), BF16),
            vmem((2, slots, plane, width), BF16),
            vmem((2, slots, plane, width), BF16),
            vmem((half * half * edge, width), F32),
            vmem((LANES, slots, half**3, width), BF16),
            vmem((LANES * slots + 1, half**3, width), F32),
            vmem((LANES, rows, 128), jnp.int32),
            pltpu.SMEM((LANES, rows, 128), jnp.int32),
            vmem((bricks + 1,) + cube, F32),
            vmem((bricks + 1,) + cube, F32),
            vmem((3 * bricks + 1,) + face, F32),
            vmem((3 * bricks + 1,) + face, F32),
            vmem((bricks, 2, plane, width), BF16),
            vmem((2, bricks, 2, plane, width), BF16),
            vmem((bricks, 2, plane, width), BF16),
            vmem((2, bricks, 2, plane, width), BF16),
            vmem((half * half * 2 * edge, width), F32),
            vmem((2, half * half, edge, width), F32),
            dma((5, 3)),
            dma((2, 2)),
            dma((2, 2)),
            dma((LANES - 1, slots)),
            dma((LANES - 1, slots)),
            dma((LANES - 1,)),
            dma((LANES - 1,)),
            dma((2, 2)),
            dma((2, 2)),
            dma(()),
        ],
        compiler_params=pltpu.CompilerParams(
            collective_id=0, has_side_effects=True, vmem_limit_bytes=60 * 1024 * 1024
        ),
    )(
        fine_nbr,
        fine_send[0],
        fine_parent,
        coarse_child,
        coarse_nbr,
        features.reshape(slots, voxels, width),
        *kernels,
    )
    return out.reshape(features.shape)


def solution(mesh):
    lead = ("groups", "gx")
    placed = (
        P(lead, None, None, None, None),
        P(lead, None),
        P(lead, None, None),
        P(lead),
        P(lead, None),
        P(lead, None),
        P(),
        P(),
        P(),
        P(),
    )
    return jax.shard_map(
        functools.partial(per_device, mesh.shape["gx"]),
        mesh=mesh,
        in_specs=placed,
        out_specs=P(lead, None, None, None, None),
        check_vma=False,
    )
```

```python
import functools

import jax
import jax.numpy as jnp
from jax import lax
from jax.experimental import pallas as pl
from jax.experimental.pallas import tpu as pltpu
from jax.sharding import PartitionSpec as P

F32 = jnp.float32
BF16 = jnp.bfloat16
LANES = 4
MESH = pl.DeviceIdType.MESH


def pick(offset, edge):
    if offset < 0:
        return slice(edge - 1, edge)
    if offset == 0:
        return slice(0, edge)
    return slice(0, 1)


def place(offset, edge, base):
    if offset < 0:
        return slice(base - 1, base)
    if offset == 0:
        return slice(base, base + edge)
    return slice(base + edge, base + edge + 1)


def kernel(
    n,
    fine_nbr,
    fine_send,
    fine_parent,
    child_ref,
    nbr_ref,
    feat_hbm,
    w1_hbm,
    w2_hbm,
    w3_hbm,
    w4_hbm,
    out_ref,
    feat,
    w1,
    w2,
    w3,
    w4,
    pad,
    cols,
    opened,
    table,
    enc,
    below,
    above,
    face_out,
    face_in,
    face_out2,
    face_in2,
    half_z,
    pooled,
    pooled_out,
    children,
    meta,
    meta_s,
    coarse,
    coarse2,
    low_x,
    high_x,
    side_out,
    side_in,
    side_out2,
    side_in2,
    spread,
    lifted,
    load_sem,
    face_send_sem,
    face_recv_sem,
    pool_send_sem,
    pool_recv_sem,
    meta_send_sem,
    meta_recv_sem,
    side_send_sem,
    side_recv_sem,
    meta_sem,
):
    slots, edge = out_ref.shape[0], enc.shape[1]
    plane = edge * edge
    width = out_ref.shape[-1]
    half = edge // 2
    block = half**3
    per = child_ref.shape[0]
    bricks = LANES * per
    me = lax.axis_index("gx")
    member = lax.rem(me, LANES)
    group = lax.div(me, LANES)

    def peer(k):
        return me - member + (member ^ k)

    width = out_ref.shape[-1]
    loads = [[pltpu.make_async_copy(feat_hbm, feat, load_sem.at[0, 0])]]
    for i, (src, dst) in enumerate(
        ((w1_hbm, w1), (w2_hbm, w2), (w3_hbm, w3), (w4_hbm, w4))
    ):
        loads.append(
            [
                pltpu.make_async_copy(
                    src.at[dx], dst.at[:, dx * width : (dx + 1) * width], load_sem.at[i + 1, dx]
                )
                for dx in range(3)
            ]
        )
    for copies in loads:
        for copy in copies:
            copy.start()

    def loaded(i):
        for copy in loads[i]:
            copy.wait()

    has_prev, has_next = me > 0, me < n - 1
    has_down, has_up = me >= LANES, me < n - LANES
    barrier = pltpu.get_barrier_semaphore()

    def greet(other):
        pl.semaphore_signal(barrier, inc=1, device_id={"gx": other}, device_id_type=MESH)

    sides = (
        (has_prev & (member == 0), me - 1),
        (has_next & (member == LANES - 1), me + 1),
        (has_down, me - LANES),
        (has_up, me + LANES),
    )
    for k in range(1, LANES):
        greet(peer(k))
    peers = LANES - 1
    for there, other in sides:
        pl.when(there)(functools.partial(greet, other))
        peers = peers + jnp.where(there, 1, 0)
    pl.semaphore_wait(barrier, peers)

    def remote(src, dst, send, recv, other):
        return pltpu.make_async_remote_copy(
            src_ref=src,
            dst_ref=dst,
            send_sem=send,
            recv_sem=recv,
            device_id={"gx": other},
            device_id_type=MESH,
        )

    def face_copies(outgoing, incoming, phase):
        up = remote(
            outgoing.at[0],
            incoming.at[0],
            face_send_sem.at[phase, 0],
            face_recv_sem.at[phase, 0],
            me + 1,
        )
        down = remote(
            outgoing.at[1],
            incoming.at[1],
            face_send_sem.at[phase, 1],
            face_recv_sem.at[phase, 1],
            me - 1,
        )
        return up, down

    def start_pair(up, up_there, down, down_there):
        pl.when(up_there)(up.start)
        pl.when(down_there)(down.start)

    def finish_pair(up, up_there, down, down_there):
        @pl.when(down_there)
        def _():
            up.wait_recv()
            down.wait_send()

        @pl.when(up_there)
        def _():
            down.wait_recv()
            up.wait_send()

    meta[member, 0:per, 0 : child_ref.shape[1]] = child_ref[...]
    meta[member, per : 2 * per, 0 : nbr_ref.shape[1]] = nbr_ref[...]

    cube = (edge, edge, edge, width)
    zero_brick = jnp.zeros(cube, F32)
    zero_plane = jnp.zeros((edge, edge, width), F32)
    table[slots] = zero_brick

    def stage_faces(outgoing, s):
        up_from = jnp.where(fine_send[0, s] >= 0, s, slots)
        down_from = jnp.where(fine_send[1, s] >= 0, s, slots)
        outgoing[0, s] = table[up_from, edge - 1].reshape(plane, width).astype(BF16)
        outgoing[1, s] = table[down_from, 0].reshape(plane, width).astype(BF16)

    loaded(0)
    for s in range(slots):
        table[s] = feat[s].astype(F32).reshape(cube)
    for s in range(slots):
        stage_faces(face_out, s)
    halo1 = face_copies(face_out, face_in, 0)
    start_pair(halo1[0], has_next, halo1[1], has_prev)
    meta_copies = [
        remote(
            meta.at[member],
            meta.at[member],
            meta_send_sem.at[k - 1],
            meta_recv_sem.at[k - 1],
            peer(k),
        )
        for k in range(1, LANES)
    ]
    for copy in meta_copies:
        copy.start()

    below[slots] = zero_plane
    above[slots] = zero_plane
    coarse[bricks] = zero_brick
    coarse2[bricks] = zero_brick
    low_x[3 * bricks] = zero_plane
    high_x[3 * bricks] = zero_plane
    children[LANES * slots] = jnp.zeros((block, width), F32)

    base = edge

    def assemble(centre, lower, upper, index, taps=range(27)):
        for t in taps:
            dx, dy, dz = t // 9 - 1, t // 3 % 3 - 1, t % 3 - 1
            at = index(t)
            ys, zs = pick(dy, edge), pick(dz, edge)
            if dx == 0:
                piece = centre[at, :, ys, zs, :]
            elif dx < 0:
                piece = lower[at, ys, zs, :][None]
            else:
                piece = upper[at, ys, zs, :][None]
            pad[place(dx, edge, 1), place(dy, edge, 1), place(dz, edge, base), :] = piece

    def product(weights, planes, rows):
        two = jnp.dot(
            cols[0 : (planes + 1) * rows, :],
            weights[:, 0 : 2 * width],
            preferred_element_type=F32,
        )
        third = jnp.dot(
            cols[2 * rows : (planes + 2) * rows, :],
            weights[:, 2 * width : 3 * width],
            preferred_element_type=F32,
        )
        total = third + two[0 : planes * rows, 0:width] + two[rows:, width : 2 * width]
        return jnp.maximum(total, 0.0).astype(BF16)

    own_taps = range(9, 18)
    far_taps = (*range(9), *range(18, 27))

    def gather_columns(x, row):
        for k in range(9):
            dy, dz = k // 3, k % 3 - 1
            piece = pad[x, dy : dy + edge, base + dz : base + dz + edge, :]
            cols[pl.ds(row, plane), k * width : (k + 1) * width] = piece.reshape(
                plane, width
            ).astype(BF16)

    def local_product(centre, j, index, weights):
        assemble(centre, None, None, index, own_taps)
        for x in range(edge):
            gather_columns(x + 1, x * plane)
        two = jnp.dot(
            cols[0 : edge * plane, :], weights[:, 0 : 2 * width], preferred_element_type=F32
        )
        third = jnp.dot(
            cols[plane : edge * plane, :],
            weights[:, 2 * width : 3 * width],
            preferred_element_type=F32,
        )
        inner = slice(plane, (edge - 1) * plane)
        middle = two[:, width : 2 * width]
        opened[j, 0] = middle[0:plane] + third[0:plane]
        opened[j, 1] = middle[(edge - 1) * plane :] + two[(edge - 2) * plane : (edge - 1) * plane, 0:width]
        total = middle[inner] + third[inner] + two[0 : (edge - 2) * plane, 0:width]
        return jnp.maximum(total, 0.0).astype(BF16)

    def outer_planes(count, lower, upper, index_of, weights, store):
        @pl.loop(0, count)
        def _(j):
            assemble(None, lower, upper, index_of(j), far_taps)
            gather_columns(0, pl.multiple_of(j * plane, plane))
            gather_columns(edge + 1, pl.multiple_of((count + j) * plane, plane))

        for side in range(2):
            added = jnp.dot(
                cols[side * count * plane : (side + 1) * count * plane, :],
                weights[:, 2 * side * width : (2 * side + 1) * width],
                preferred_element_type=F32,
            )
            for j in range(count):
                total = opened[j, side] + added[j * plane : (j + 1) * plane]
                store(j, side * (edge - 1), jnp.maximum(total, 0.0).astype(BF16))

    def fine_index(b):
        def index(t):
            at = fine_nbr[b, t]
            return jnp.where(at >= 0, at, slots)

        return index

    def take_faces(incoming):
        for s in range(slots):
            below[s] = incoming[0, s].astype(F32).reshape(edge, edge, width)
            above[s] = incoming[1, s].astype(F32).reshape(edge, edge, width)

    loaded(1)
    face = (edge, edge, width)
    cells = half * half

    def pool_copy(k, b):
        if b is None:
            source, at = pooled_out.at[member], slots
        else:
            source, at = pooled.at[member, b], b
        return remote(
            source, source, pool_send_sem.at[k - 1, at], pool_recv_sem.at[k - 1, at], peer(k)
        )

    def pool(value, count):
        pairs = value.reshape(count, 2, half, 2, edge, width)
        summed = (pairs[:, 0, :, 0] + pairs[:, 0, :, 1]) + (pairs[:, 1, :, 0] + pairs[:, 1, :, 1])
        half_z[0 : count * half * edge, :] = summed.reshape(count * half * edge, width)
        even = half_z[pl.ds(0, count * cells, stride=2), :]
        odd = half_z[pl.ds(1, count * cells, stride=2), :]
        return ((even + odd) * 0.125).astype(BF16)

    @pl.loop(0, slots)
    def _(b):
        value = local_product(table, b, fine_index(b), w1).astype(F32)
        value = value.reshape((edge - 2,) + face)
        enc[b, 1 : edge - 1] = value
        pooled[member, b] = pool(value[1 : edge - 3], half - 2)
        for k in range(1, LANES):
            pool_copy(k, b).start()

    finish_pair(halo1[0], has_next, halo1[1], has_prev)
    take_faces(face_in)

    def store_enc(b, x, value):
        enc[b, x] = value.astype(F32).reshape(face)

    outer_planes(slots, below, above, fine_index, w1, store_enc)
    for b in range(slots):
        pooled_out[member, b, 0:cells] = pool(enc[b, 0:2], 1)
        pooled_out[member, b, cells : 2 * cells] = pool(enc[b, edge - 2 : edge], 1)
    for k in range(1, LANES):
        pool_copy(k, None).start()

    for copy in meta_copies:
        copy.wait()
    to_smem = pltpu.make_async_copy(meta, meta_s, meta_sem)
    to_smem.start()
    for k in range(1, LANES):
        for b in (*range(slots), None):
            pool_copy(k, b).wait()
    to_smem.wait()
    for lane in range(LANES):
        for s in range(slots):
            at = lane * slots + s
            children[at, cells : block - cells] = pooled[lane, s].astype(F32)
            children[at, 0:cells] = pooled_out[lane, s, 0:cells].astype(F32)
            children[at, block - cells : block] = pooled_out[lane, s, cells : 2 * cells].astype(F32)

    def owner_of(value):
        value = jnp.maximum(value, 0)
        return lax.div(value, per), lax.rem(value, per)

    @pl.loop(0, bricks)
    def _(j):
        lane, slot = lax.div(j, per), lax.rem(j, per)
        for o in range(8):
            child = meta_s[lane, slot, o]
            safe = jnp.maximum(child, 0)
            at = lax.rem(lax.div(safe, slots), LANES) * slots + lax.rem(safe, slots)
            at = jnp.where(child >= 0, at, LANES * slots)
            ox, oy, oz = o // 4 * half, o // 2 % 2 * half, o % 2 * half
            for x in range(half):
                for y in range(half):
                    row = (x * half + y) * half
                    coarse[j, ox + x, oy + y, oz : oz + half, :] = children[
                        at, row : row + half, :
                    ]

    def side_copies(outgoing, incoming, phase):
        up = remote(
            outgoing,
            incoming.at[0],
            side_send_sem.at[phase, 0],
            side_recv_sem.at[phase, 0],
            me + LANES,
        )
        down = remote(
            outgoing,
            incoming.at[1],
            side_send_sem.at[phase, 1],
            side_recv_sem.at[phase, 1],
            me - LANES,
        )
        return up, down

    def coarse_index(lane, slot, live):
        def index(t):
            value = meta_s[lane, per + slot, t]
            there = (value >= 0) & live
            device, at = owner_of(value)
            at = lax.rem(device, LANES) * per + at
            if t // 9 == 1:
                return jnp.where(there, at, bricks)
            at = at + (lax.div(device, LANES) - group + 1) * bricks
            at = jnp.minimum(jnp.maximum(at, 0), 3 * bricks)
            return jnp.where(there, at, 3 * bricks)

        return index

    def send_sides(source, outgoing, incoming, phase):
        for j in range(bricks):
            first, last = source[j, 0], source[j, edge - 1]
            low_x[bricks + j] = first
            high_x[bricks + j] = last
            outgoing[j, 0] = first.reshape(plane, width).astype(BF16)
            outgoing[j, 1] = last.reshape(plane, width).astype(BF16)
        up, down = side_copies(outgoing, incoming, phase)
        start_pair(up, has_up, down, has_down)
        return up, down

    def take_sides(copies, incoming):
        finish_pair(copies[0], has_up, copies[1], has_down)
        for side, start in ((0, 0), (1, 2 * bricks)):
            for j in range(bricks):
                low_x[start + j] = incoming[side, j, 0].astype(F32).reshape(edge, edge, width)
                high_x[start + j] = incoming[side, j, 1].astype(F32).reshape(edge, edge, width)

    def group_index(j):
        return coarse_index(lax.div(j, per), lax.rem(j, per), True)

    face = (edge, edge, width)
    copies = send_sides(coarse, side_out, side_in, 0)
    loaded(2)

    @pl.loop(0, bricks)
    def _(j):
        value = local_product(coarse, j, group_index(j), w2).astype(F32)
        coarse2[j, 1 : edge - 1] = value.reshape((edge - 2,) + face)

    take_sides(copies, side_in)

    def store_coarse(j, x, value):
        coarse2[j, x] = value.astype(F32).reshape(face)

    outer_planes(bricks, high_x, low_x, group_index, w2, store_coarse)
    copies = send_sides(coarse2, side_out2, side_in2, 1)
    loaded(3)

    part = half * edge
    strip = slots * part

    def quarter(s, taps, planes):
        parent = fine_parent[s]
        safe = jnp.maximum(parent, 0)
        device, slot = owner_of(lax.div(safe, 8))
        octant = lax.rem(safe, 8)
        ox = lax.div(octant, 4) * half
        oy = lax.rem(lax.div(octant, 2), 2) * half
        index = coarse_index(lax.rem(device, LANES), slot, parent >= 0)
        assemble(coarse2, high_x, low_x, index, taps)
        for x in planes:
            start = pl.multiple_of(x * strip + s * part, part)
            for k in range(9):
                dy, dz = k // 3, k % 3 - 1
                piece = pad[ox + x, pl.ds(oy + dy, half), base + dz : base + dz + edge, :]
                cols[pl.ds(start, part), k * width : (k + 1) * width] = piece.reshape(
                    part, width
                ).astype(BF16)

    @pl.loop(0, slots)
    def _(s):
        quarter(s, own_taps, range(1, half + 1))

    take_sides(copies, side_in2)

    @pl.loop(0, slots)
    def _(s):
        quarter(s, range(27), (0, half + 1))

    parents = product(w3, half, strip).astype(F32).reshape(half, slots, part, width)

    for s in range(slots):
        oz = lax.rem(jnp.maximum(fine_parent[s], 0), 2)
        piece = parents[:, s].reshape(half * half * edge, width)
        spread[pl.ds(0, half * half * edge, stride=2), :] = piece
        spread[pl.ds(1, half * half * edge, stride=2), :] = piece
        for z in range(2):
            for row in range(half * half):
                start = row * 2 * edge + z * edge
                lifted[z, row] = spread[start : start + edge, :]
        for x in range(half):
            for y in range(half):
                up = lifted[oz, x * half + y]
                for xx in range(2):
                    for yy in range(2):
                        value = enc[s, 2 * x + xx, 2 * y + yy] + up
                        table[s, 2 * x + xx, 2 * y + yy] = value.astype(BF16).astype(F32)
        stage_faces(face_out2, s)
    halo2 = face_copies(face_out2, face_in2, 1)
    start_pair(halo2[0], has_next, halo2[1], has_prev)
    loaded(4)

    @pl.loop(0, slots)
    def _(b):
        value = local_product(table, b, fine_index(b), w4)
        out_ref[b, plane : (edge - 1) * plane, :] = value

    finish_pair(halo2[0], has_next, halo2[1], has_prev)
    take_faces(face_in2)

    def store_fine(b, x, value):
        out_ref[b, x * plane : (x + 1) * plane, :] = value

    outer_planes(slots, below, above, fine_index, w4, store_fine)


def per_device(
    n,
    features,
    fine_nbr,
    fine_send,
    fine_parent,
    coarse_child,
    coarse_nbr,
    enc_fine_w,
    enc_coarse_w,
    dec_coarse_w,
    dec_fine_w,
):
    slots, edge, width = features.shape[0], features.shape[1], features.shape[-1]
    per = coarse_nbr.shape[0]
    bricks = LANES * per
    half = edge // 2
    plane = edge * edge
    voxels = edge**3
    strip = slots * half * edge
    rows = -(-2 * per // 8) * 8
    kernels = [
        w.reshape(3, 9 * width, width)
        for w in (enc_fine_w, enc_coarse_w, dec_coarse_w, dec_fine_w)
    ]
    vmem = pltpu.VMEM
    smem_spec = pl.BlockSpec(memory_space=pltpu.SMEM)
    vmem_spec = pl.BlockSpec(memory_space=pltpu.VMEM)
    any_spec = pl.BlockSpec(memory_space=pl.ANY)
    cube = (edge, edge, edge, width)
    face = (edge, edge, width)
    dma = pltpu.SemaphoreType.DMA
    out = pl.pallas_call(
        functools.partial(kernel, n),
        out_shape=jax.ShapeDtypeStruct((slots, voxels, width), BF16),
        in_specs=[smem_spec] * 3 + [vmem_spec] * 2 + [any_spec] * 5,
        out_specs=vmem_spec,
        scratch_shapes=[
            vmem((slots, voxels, width), BF16),
            *[vmem((9 * width, 3 * width), BF16)] * 4,
            vmem((edge + 2, edge + 2, 3 * edge, width), F32),
            vmem((max((edge + 2) * plane, (half + 2) * strip, 2 * max(slots, bricks) * plane), 9 * width), BF16),
            vmem((max(slots, bricks), 2, plane, width), F32),
            vmem((slots + 1,) + cube, F32),
            vmem((slots,) + cube, F32),
            vmem((slots + 1,) + face, F32),
            vmem((slots + 1,) + face, F32),
            vmem((2, slots, plane, width), BF16),
            vmem((2, slots, plane, width), BF16),
            vmem((2, slots, plane, width), BF16),
            vmem((2, slots, plane, width), BF16),
            vmem((half * half * edge, width), F32),
            vmem((LANES, slots, (half - 2) * half**2, width), BF16),
            vmem((LANES, slots, 2 * half**2, width), BF16),
            vmem((LANES * slots + 1, half**3, width), F32),
            vmem((LANES, rows, 128), jnp.int32),
            pltpu.SMEM((LANES, rows, 128), jnp.int32),
            vmem((bricks + 1,) + cube, F32),
            vmem((bricks + 1,) + cube, F32),
            vmem((3 * bricks + 1,) + face, F32),
            vmem((3 * bricks + 1,) + face, F32),
            vmem((bricks, 2, plane, width), BF16),
            vmem((2, bricks, 2, plane, width), BF16),
            vmem((bricks, 2, plane, width), BF16),
            vmem((2, bricks, 2, plane, width), BF16),
            vmem((half * half * 2 * edge, width), F32),
            vmem((2, half * half, edge, width), F32),
            dma((5, 3)),
            dma((2, 2)),
            dma((2, 2)),
            dma((LANES - 1, slots + 1)),
            dma((LANES - 1, slots + 1)),
            dma((LANES - 1,)),
            dma((LANES - 1,)),
            dma((2, 2)),
            dma((2, 2)),
            dma(()),
        ],
        compiler_params=pltpu.CompilerParams(
            collective_id=0, has_side_effects=True, vmem_limit_bytes=60 * 1024 * 1024
        ),
    )(
        fine_nbr,
        fine_send[0],
        fine_parent,
        coarse_child,
        coarse_nbr,
        features.reshape(slots, voxels, width),
        *kernels,
    )
    return out.reshape(features.shape)


def solution(mesh):
    lead = ("groups", "gx")
    placed = (
        P(lead, None, None, None, None),
        P(lead, None),
        P(lead, None, None),
        P(lead),
        P(lead, None),
        P(lead, None),
        P(),
        P(),
        P(),
        P(),
    )
    return jax.shard_map(
        functools.partial(per_device, mesh.shape["gx"]),
        mesh=mesh,
        in_specs=placed,
        out_specs=P(lead, None, None, None, None),
        check_vma=False,
    )
```
